1024 devices in a mesh: wide: 32 (over x, z_lo), narrow: 32 (over y, z_hi, core).
Axes of the slice: x: 4, y: 4, z: 32 (z_hi: 4, z_lo: 8; z = z_hi * 8 + z_lo), core: 2. Of those that a mesh axis runs over, the one named last changes fastest.
Arguments:
- state: float32 [32, 512, 512], P('narrow'), may hold values from -1.5 to 1.5
- left_env: float32 [32, 32, 512, 512], P('wide', 'narrow')
- right_env: float32 [32, 32, 512, 512], P('wide', 'narrow')
- left_sizes: int32 [32], replicated, may hold values from 1 to 512, 12288 in all
- right_sizes: int32 [32], replicated, may hold values from 1 to 512, 12288 in all
- channel_charge: int32 [32], P('wide'), may hold values from 0 to 2
Outputs:
- lanczos_vector: float32 [32, 512, 512], P('narrow', 'wide')
- alpha: float32 [], replicated
The draws below stay inside these ranges and needn't reach their ends.
Inputs may be any that keep to these rules, and one draw needn't show every extreme that they name: `left_sizes`: basis states of each left sector; they add up to 12288, and some sector has exactly 512. `right_sizes`: basis states of each right sector; they add up to 12288, and some sector has exactly 512. `channel_charge`: 0 lowers the sector by one, 1 keeps it, 2 raises it by one.
All inputs are finite; a program needn't handle non-finite values.
Results may differ from the reference program's by a relative error of at most 0.0003.
Values sent between devices are 32-bit elements; how exact they have to be, the bound alone decides.
A program may use at most 32 MiB of HBM per device.

```python
import math
import jax
import jax.numpy as jnp
import numpy as np
from jax import lax

W = 32
S = 512
K = 32
BOND = 12288


def draw_left_env(key, part):
    shape = (W, K, S, S)
    rowidx = lax.broadcasted_iota(jnp.int32, shape, 2)
    colidx = lax.broadcasted_iota(jnp.int32, shape, 3)
    diagonal = (rowidx == colidx).astype(jnp.float32)
    sub = jax.random.fold_in(key, 11)
    noise = jax.random.normal(sub, shape, jnp.float32)
    return noise * S ** (-0.5) + diagonal


def draw_right_env(key, part):
    shape = (W, K, S, S)
    rowidx = lax.broadcasted_iota(jnp.int32, shape, 2)
    colidx = lax.broadcasted_iota(jnp.int32, shape, 3)
    diagonal = (rowidx == colidx).astype(jnp.float32)
    sub = jax.random.fold_in(key, 23)
    noise = jax.random.normal(sub, shape, jnp.float32)
    return noise * S ** (-0.5) + diagonal


def set_ends(array, own_key, low, largest):
    longest = array.shape.index(max(array.shape))
    spots = []
    for shift in (0, 1):
        where = [jax.random.randint(jax.random.fold_in(own_key, axis), (), 0, length) for axis, length in enumerate(array.shape)]
        where[longest] = (where[longest] + shift) % array.shape[longest]
        spots.append(tuple(where))
    return array.at[spots[0]].set(low).at[spots[1]].set(largest)


def levels(rng, extent, cuts, smallest, top_value):
    level, own = 1.0, jax.random.fold_in(rng, 6)
    for axis_at, parts in cuts:
        heights = jnp.exp(jax.random.uniform(jax.random.fold_in(own, axis_at), (parts,), jnp.float32, smallest / len(cuts), top_value / len(cuts)))
        level = level * jnp.repeat(heights, extent[axis_at] // parts).reshape([-1 if axis == axis_at else 1 for axis in range(len(extent))])
    return level


def split_up(count, total, limit, skew):
    loads = [(1 << 20) // math.isqrt(rank ** skew) + 1 for rank in range(2, count + 1)]
    rest, holding = total - limit - (count - 1), [1] * (count - 1)
    while rest > 0:
        free = [i for i in range(count - 1) if holding[i] < limit]
        pool, left = sum([loads[i] for i in free]), rest
        for i in free:
            extra = min(limit - holding[i], max(1, left * loads[i] // pool), rest)
            holding[i] = holding[i] + extra
            rest = rest - extra
    return np.array([limit] + holding)


def ragged_sizes(own_key, count, total, bound, skew):
    if count == 2:
        one = jax.random.randint(own_key, (), max(1, total - bound), min(bound, total - 1) + 1)
        return jnp.stack([one, total - one])
    lengths = jnp.asarray(split_up(count, total, bound, skew), jnp.int32)
    pairs = (count - 1) // 2
    giver, receiver = lengths[1:1 + 2 * pairs:2], lengths[2:2 + 2 * pairs:2]
    room = jnp.minimum(giver - 1, bound - receiver)
    passed = jax.random.randint(jax.random.fold_in(own_key, 1), (pairs,), 0, 1 << 20) % (room + 1)
    lengths = lengths.at[1:1 + 2 * pairs:2].set(giver - passed).at[2:2 + 2 * pairs:2].set(receiver + passed)
    return lengths[jax.random.permutation(jax.random.fold_in(own_key, 2), count)]


def scatter_about(rng, extent, width, reach, pieces=(), kind=jnp.bfloat16):
    result = jax.random.normal(rng, extent, jnp.float32) * width
    if len(pieces) > 0:
        result = levels(rng, extent, pieces, -0.22, 0.18) * result
    return jnp.clip(result, min=-reach, max=reach).astype(kind)


def setup_inputs(seed: int = 0) -> dict:
    splits = jax.random.split(jax.random.key(seed), 7)
    state = scatter_about(splits[0], (K, S, S), 0.25, 1.5, ((0, 32),), jnp.float32)
    left_env = draw_left_env(jax.random.fold_in(splits[6], 71), 0)
    right_env = draw_right_env(jax.random.fold_in(splits[6], 71), 0)
    left_sizes = ragged_sizes(splits[3], K, BOND, S, 2).astype(jnp.int32)
    right_sizes = ragged_sizes(splits[4], K, BOND, S, 1).astype(jnp.int32)
    channel_charge = set_ends(jax.random.randint(splits[5], (W,), 0, 3), jax.random.fold_in(splits[5], 1), 0, 2).astype(jnp.int32)
    return {"state": state, "left_env": left_env, "right_env": right_env, "left_sizes": left_sizes, "right_sizes": right_sizes, "channel_charge": channel_charge}


def valid_table(sizes):
    positions = jnp.arange(S, dtype=jnp.int32)
    return (positions[None, :] < sizes[:, None]).astype(jnp.float32)


def reference(state, left_env, right_env, left_sizes, right_sizes, channel_charge):
    left_ok = valid_table(left_sizes)
    right_ok = valid_table(right_sizes)
    psi = state * left_ok[:, :, None] * right_ok[:, None, :]
    sectors = jnp.arange(K, dtype=jnp.int32)

    def one_channel(total, inputs):
        lenv, renv, charge = inputs
        source = sectors - (charge - 1)
        inside = ((source >= 0) & (source < K)).astype(jnp.float32)
        clipped = jnp.clip(source, 0, K - 1).astype(jnp.int32)
        psi_src = psi[clipped] * inside[:, None, None]
        left_src = left_ok[clipped] * inside[:, None]
        right_src = right_ok[clipped] * inside[:, None]
        lmat = lenv * left_ok[:, :, None] * left_src[:, None, :]
        rmat = renv * right_ok[:, :, None] * right_src[:, None, :]
        inner = jnp.einsum("kab,kbc->kac", lmat, psi_src, precision=lax.Precision.HIGHEST)
        term = jnp.einsum("kac,kdc->kad", inner, rmat, precision=lax.Precision.HIGHEST)
        return total + term, None

    hpsi, unused = lax.scan(one_channel, jnp.zeros((K, S, S), jnp.float32), (left_env, right_env, channel_charge))
    alpha = jnp.sum(psi * hpsi) / jnp.sum(psi * psi)
    return hpsi - alpha * psi, alpha
```

```python
import functools

import jax
import jax.numpy as jnp
from jax import lax
from jax.experimental import pallas as pl
from jax.experimental.pallas import tpu as pltpu
from jax.sharding import PartitionSpec as P

MESH = pl.DeviceIdType.MESH
F32 = jnp.float32
BF16 = jnp.bfloat16

NX = 4
NJ = 8
NQ = 4
NR = 4
NC = 2


def split(v):
    high = v.astype(BF16)
    return high, (v - high.astype(F32)).astype(BF16)


def product(ah, al, bh, bl, dims):
    dot = functools.partial(
        lax.dot_general, dimension_numbers=(dims, ((), ())), preferred_element_type=F32
    )
    return dot(ah, bh) + (dot(ah, bl) + dot(al, bh))


def kernel(
    state, left, right, lsizes, rsizes, charge,
    out, alpha_out,
    own, lenv, renv, near, far, ph, plo, rh, rl, term,
    from_left, from_right, zsum, zrecv, g1, g2, g3,
    local_sem, send_sem, recv_sem,
):
    size = own.shape[0]
    band = size // (NX * NJ)
    block = band * NJ
    half = block // 2
    quarter = half // 2
    w = lax.axis_index("wide")
    n = lax.axis_index("narrow")
    x, j = w // NJ, w % NJ
    q, r, c = n // (NR * NC), (n // NC) % NR, n % NC
    total_n = NQ * NR * NC

    def at_x(step):
        return (lax.rem(x + step, NX) * NJ + j, n)

    def at_j(other):
        return (x * NJ + other, n)

    def at_qr(step):
        qr = lax.rem(q * NR + r + step, NQ * NR)
        return (w, qr * NC + c)

    def at_xc(step):
        xc = lax.rem(x * NC + c + step, NX * NC)
        return ((xc // NC) * NJ + j, (q * NR + r) * NC + xc % NC)

    sibling = (w, n + 1 - 2 * c)
    across = (w, lax.rem(n + 2 * c - 1 + total_n, total_n))

    own_copy = pltpu.make_async_copy(state, own, local_sem.at[0])
    left_copy = pltpu.make_async_copy(left, lenv, local_sem.at[1])
    right_copy = pltpu.make_async_copy(right, renv, local_sem.at[2])
    right_copy.start()
    own_copy.start()
    left_copy.start()

    barrier = pltpu.get_barrier_semaphore()
    partners = (
        [across]
        + [at_j(lax.rem(j + s, NJ)) for s in range(1, NJ)]
        + [at_xc(s) for s in range(1, NX * NC)]
        + [at_qr(s) for s in range(1, NQ * NR)]
    )
    for partner in partners:
        pl.semaphore_signal(barrier, inc=1, device_id=partner, device_id_type=MESH)
    pl.semaphore_wait(barrier, len(partners))

    started = []

    def push(src, dst, device):
        i = len(started)
        copy = pltpu.make_async_remote_copy(
            src_ref=src, dst_ref=dst, send_sem=send_sem.at[i], recv_sem=recv_sem.at[i],
            device_id=device, device_id_type=MESH,
        )
        copy.start()
        started.append(copy)
        return copy

    pos = (j % 2) * 4 + (j // 2 % 2) * 2 + j // 4
    base = x * block

    def rows(start, count):
        return pl.ds(pl.multiple_of(start, 8), count)

    shard = rows(base + pos * band, band)
    cross = push(state.at[shard], far.at[shard], across)
    nearby = push(state, near, sibling)

    right_copy.wait()
    slab = 32

    @pl.loop(0, size // slab)
    def _(i):
        at = rows(i * slab, slab)
        rh[at], rl[at] = split(renv[at])

    own_copy.wait()
    rows_own, cols_own = lsizes[n], rsizes[n]

    def masked(values, first, rlimit, climit):
        rid = lax.broadcasted_iota(jnp.int32, values.shape, 0) + first
        cid = lax.broadcasted_iota(jnp.int32, values.shape, 1)
        return jnp.where((rid < rlimit) & (cid < climit), values, 0.0)

    def lanes(values):
        s = jnp.sum(values, axis=0, keepdims=True)
        return s[:, 0:128] + s[:, 128:256] + s[:, 256:384] + s[:, 384:512]

    def square(i, total):
        at = rows(i * slab, slab)
        psi = masked(own[at], i * slab, rows_own, cols_own)
        own[at] = psi
        return total + lanes(psi * psi)

    den = lax.fori_loop(0, size // slab, square, jnp.zeros((1, 128), F32))
    den = jnp.where(w == 0, den, 0.0)

    def part(xb, start, count):
        return rows(xb * block + start, count)

    x1, x2, x3 = lax.rem(x + 1, NX), lax.rem(x + 2, NX), lax.rem(x + 3, NX)

    cross.wait_recv()
    first = push(far.at[shard], far.at[shard], at_j(j + 4 - 8 * (j // 4)))
    first.wait_recv()
    at2 = rows(base + (pos // 2) * 2 * band, 2 * band)
    second = push(far.at[at2], far.at[at2], at_j(j + 2 - 4 * (j // 2 % 2)))
    second.wait_recv()
    lo = (pos // 4) * half
    hi = half - lo
    at3 = rows(base + lo, half)
    third = push(far.at[at3], far.at[at3], at_j(j + 1 - 2 * (j % 2)))
    right_lo = push(far.at[at3], far.at[at3], at_x(1))
    left_lo = push(far.at[at3], far.at[at3], at_x(3))
    third.wait_recv()
    at4 = rows(base + hi, half)
    right_hi = push(far.at[at4], far.at[at4], at_x(1))
    left_hi = push(far.at[at4], far.at[at4], at_x(3))
    right_lo.wait_recv()
    piece = part(x3, lo, quarter)
    relay_right_lo = push(far.at[piece], far.at[piece], at_x(1))
    left_lo.wait_recv()
    piece = part(x1, lo + quarter, quarter)
    relay_left_lo = push(far.at[piece], far.at[piece], at_x(3))
    right_hi.wait_recv()
    piece = part(x3, hi, quarter)
    relay_right_hi = push(far.at[piece], far.at[piece], at_x(1))
    left_hi.wait_recv()
    piece = part(x1, hi + quarter, quarter)
    relay_left_hi = push(far.at[piece], far.at[piece], at_x(3))
    nearby.wait_recv()
    left_copy.wait()
    relay_right_lo.wait_recv()
    relay_left_lo.wait_recv()
    relay_right_hi.wait_recv()
    relay_left_hi.wait_recv()

    shift = charge[0] - 1
    source = n - shift
    clipped = jnp.clip(source, 0, total_n - 1)
    inside = (source == clipped).astype(jnp.int32)
    rows_src, cols_src = lsizes[clipped] * inside, rsizes[clipped] * inside
    toward = shift * (1 - 2 * c)

    @pl.loop(0, size // slab)
    def _(i):
        at = rows(i * slab, slab)
        took = jnp.where(toward == 1, far[at], jnp.where(toward == 0, own[at], near[at]))
        ph[at], plo[at] = split(masked(took, i * slab, rows_src, cols_src))

    num = jnp.zeros((1, 128), F32)

    def compute(xb, num):
        at = part(xb, 0, block)
        lh, ll = split(lenv[at])
        inner = product(lh, ll, ph[...], plo[...], ((1,), (0,)))
        ih, il = split(inner)
        t = product(ih, il, rh[...], rl[...], ((1,), (1,)))
        t = masked(t, xb * block, rows_own, cols_own)
        term[at] = t
        return num + lanes(t * own[at])

    num = compute(x2, num)
    r1 = push(term.at[part(x2, 0, half)], from_left.at[0], at_x(1))
    l1 = push(term.at[part(x2, half, half)], from_right.at[0], at_x(3))
    num = compute(x1, num)
    r2 = push(term.at[part(x1, half, half)], from_left.at[1], at_x(1))
    num = compute(x3, num)
    l2 = push(term.at[part(x3, 0, half)], from_right.at[1], at_x(3))
    num = compute(x, num)

    g1[j] = jnp.concatenate([num, den], axis=1)
    c1 = [push(g1.at[j], g1.at[j], at_j(lax.rem(j + s, NJ))) for s in range(1, NJ)]

    r1.wait_recv()
    at = part(x1, 0, half)
    term[at] += from_left[0]
    r3 = push(term.at[at], from_left.at[2], at_x(1))
    l1.wait_recv()
    at = part(x3, half, half)
    term[at] += from_right[0]
    l3 = push(term.at[at], from_right.at[2], at_x(3))

    for copy in c1:
        copy.wait_recv()
    xc = x * NC + c
    s1 = g1[0]
    for i in range(1, NJ):
        s1 = s1 + g1[i]
    g2[xc] = s1
    c2 = [push(g2.at[xc], g2.at[xc], at_xc(s)) for s in range(1, NX * NC)]

    r2.wait_recv()
    l2.wait_recv()
    r3.wait_recv()
    zsum[0:half] = term[part(x, 0, half)] + from_left[2] + from_right[1]
    l3.wait_recv()
    zsum[half:block] = term[part(x, half, half)] + from_left[1] + from_right[2]
    zs = []
    for s in (4, 3, 5, 2, 6, 1, 7):
        other = lax.rem(j + s, NJ)
        zs.append(push(zsum.at[rows(other * band, band)], zrecv.at[j], at_j(other)))

    for copy in c2:
        copy.wait_recv()
    qr = q * NR + r
    s2 = g2[0]
    for i in range(1, NX * NC):
        s2 = s2 + g2[i]
    g3[qr] = s2
    c3 = [push(g3.at[qr], g3.at[qr], at_qr(s)) for s in range(1, NQ * NR)]

    zrecv[j] = zsum[rows(j * band, band)]
    for copy in c3:
        copy.wait_recv()
    s3 = g3[0]
    for i in range(1, NQ * NR):
        s3 = s3 + g3[i]
    alpha = jnp.sum(s3[:, 0:128], axis=1, keepdims=True) / jnp.sum(
        s3[:, 128:256], axis=1, keepdims=True
    )
    alpha_out[...] = alpha
    for copy in zs:
        copy.wait_recv()
    share = zrecv[0]
    for i in range(1, NJ):
        share = share + zrecv[i]
    out[...] = share - alpha * own[rows(w * band, band)]
    for copy in started:
        copy.wait_send()


COPIES = 2 + 3 + 8 + 6 + (NJ - 1) * 2 + (NX * NC - 1) + (NQ * NR - 1)


def per_device(state, left_env, right_env, left_sizes, right_sizes, channel_charge):
    size = state.shape[1]
    band = size // (NX * NJ)
    block = band * NJ
    hbm = pl.BlockSpec(memory_space=pl.ANY)
    smem = pl.BlockSpec(memory_space=pltpu.SMEM)
    vmem = pl.BlockSpec(memory_space=pltpu.VMEM)
    full = (size, size)
    share, alpha = pl.pallas_call(
        kernel,
        out_shape=(
            jax.ShapeDtypeStruct((band, size), F32),
            jax.ShapeDtypeStruct((1, 1), F32),
        ),
        in_specs=[hbm, hbm, hbm, smem, smem, smem],
        out_specs=(vmem, vmem),
        scratch_shapes=[
            pltpu.VMEM(full, F32),
            pltpu.VMEM(full, F32),
            pltpu.VMEM(full, F32),
            pltpu.VMEM(full, F32),
            pltpu.VMEM(full, F32),
            pltpu.VMEM(full, BF16),
            pltpu.VMEM(full, BF16),
            pltpu.VMEM(full, BF16),
            pltpu.VMEM(full, BF16),
            pltpu.VMEM(full, F32),
            pltpu.VMEM((3, block // 2, size), F32),
            pltpu.VMEM((3, block // 2, size), F32),
            pltpu.VMEM((block, size), F32),
            pltpu.VMEM((NJ, band, size), F32),
            pltpu.VMEM((NJ, 1, 256), F32),
            pltpu.VMEM((NX * NC, 1, 256), F32),
            pltpu.VMEM((NQ * NR, 1, 256), F32),
            pltpu.SemaphoreType.DMA((3,)),
            pltpu.SemaphoreType.DMA((COPIES,)),
            pltpu.SemaphoreType.DMA((COPIES,)),
        ],
        compiler_params=pltpu.CompilerParams(
            collective_id=0, has_side_effects=True, vmem_limit_bytes=60 << 20
        ),
    )(state[0], left_env[0, 0], right_env[0, 0], left_sizes, right_sizes, channel_charge)
    return share[None], alpha[0, 0]


def solution(mesh):
    placed = (
        P("narrow", None, None),
        P("wide", "narrow", None, None),
        P("wide", "narrow", None, None),
        P(),
        P(),
        P("wide"),
    )
    return jax.shard_map(
        per_device,
        mesh=mesh,
        in_specs=placed,
        out_specs=(P("narrow", "wide", None), P()),
        check_vma=False,
    )
```

```python
import functools

import jax
import jax.numpy as jnp
from jax import lax
from jax.experimental import pallas as pl
from jax.experimental.pallas import tpu as pltpu
from jax.sharding import PartitionSpec as P

MESH = pl.DeviceIdType.MESH
F32 = jnp.float32
BF16 = jnp.bfloat16

NX = 4
NJ = 8
NQ = 4
NR = 4
NC = 2
LANES = 128
COPIES = 72


def split(v):
    high = v.astype(BF16)
    return high, (v - high.astype(F32)).astype(BF16)


def product(ah, al, bh, bl):
    dot = functools.partial(jnp.dot, preferred_element_type=F32)
    return dot(ah, bh) + (dot(ah, bl) + dot(al, bh))


def kernel(
    state, left, right, lsizes, rsizes, charge,
    result,
    own, lenv, renv, near, far, lh, ll, rh, rl, ph, plo, ih, il, term,
    from_x, zsum, zrecv, g1, g2, g3,
    local_sem, send_sem, recv_sem,
):
    size = own.shape[0]
    band = size // (NX * NJ)
    block = band * NJ
    pair = 2 * band
    tall = size // NJ
    w = lax.axis_index("wide")
    n = lax.axis_index("narrow")
    x, j = w // NJ, w % NJ
    h, i = j // 4, j % 4
    q, r, c = n // (NR * NC), (n // NC) % NR, n % NC
    total_n = NQ * NR * NC

    def at_x(step):
        return (lax.rem(x + step, NX) * NJ + j, n)

    def at_j(other):
        return (x * NJ + other, n)

    def at_qr(step):
        qr = lax.rem(q * NR + r + step, NQ * NR)
        return (w, qr * NC + c)

    def at_xc(step):
        xc = lax.rem(x * NC + c + step, NX * NC)
        return ((xc // NC) * NJ + j, (q * NR + r) * NC + xc % NC)

    over = lax.rem(n + 2 * c - 1 + total_n, total_n)
    sibling = (w, n + 1 - 2 * c)
    across = (w, over)
    across_four = (x * NJ + (1 - h) * 4 + i, over)
    quad = [i + 1 - 2 * (i % 2), i + 2 - 4 * (i // 2), 3 - i]

    own_copy = pltpu.make_async_copy(state, own, local_sem.at[0])
    left_copy = pltpu.make_async_copy(left, lenv, local_sem.at[1])
    right_copy = pltpu.make_async_copy(right, renv, local_sem.at[2])

    barrier = pltpu.get_barrier_semaphore()
    partners = (
        [across, across_four]
        + [at_qr(s) for s in range(1, NQ * NR)]
        + [at_j(lax.rem(j + s, NJ)) for s in range(1, NJ)]
        + [at_xc(s) for s in range(1, NX * NC)]
    )
    for partner in partners:
        pl.semaphore_signal(barrier, inc=1, device_id=partner, device_id_type=MESH)
    right_copy.start()
    own_copy.start()
    left_copy.start()
    pl.semaphore_wait(barrier, len(partners))

    started = []

    def push(src, dst, device):
        i = len(started)
        copy = pltpu.make_async_remote_copy(
            src_ref=src, dst_ref=dst, send_sem=send_sem.at[i], recv_sem=recv_sem.at[i],
            device_id=device, device_id_type=MESH,
        )
        copy.start()
        started.append(copy)
        return copy

    def rows(start, count):
        return pl.ds(pl.multiple_of(start, 8), count)

    def cols(xb):
        return pl.ds(pl.multiple_of(xb * LANES, LANES), LANES)

    piece = state.at[rows(j * tall, tall), cols(x)]
    cross = push(piece, far.at[h, i, :, cols(x)], across)
    cross_four = push(piece, far.at[h, i, :, cols(x)], across_four)
    nearby = push(state, near, sibling)

    slab = 32
    right_copy.wait()
    for t in range(size // LANES):
        at = pl.ds(t * LANES, LANES)
        rh[at, :], rl[at, :] = split(renv[:, at].T)

    left_copy.wait()

    @pl.loop(0, size // slab)
    def _(t):
        at = rows(t * slab, slab)
        lh[at], ll[at] = split(lenv[at])

    own_copy.wait()
    rows_own, cols_own = lsizes[n], rsizes[n]

    def masked(values, first, across_first, rlimit, climit):
        rid = lax.broadcasted_iota(jnp.int32, values.shape, 0) + first
        cid = lax.broadcasted_iota(jnp.int32, values.shape, 1) + across_first
        return jnp.where((rid < rlimit) & (cid < climit), values, 0.0)

    def lanes(values):
        s = jnp.sum(values, axis=0, keepdims=True)
        return s[:, 0:128] + s[:, 128:256] + s[:, 256:384] + s[:, 384:512]

    def square(t, total):
        at = rows(t * slab, slab)
        psi = masked(own[at], t * slab, 0, rows_own, cols_own)
        own[at] = psi
        return total + lanes(psi * psi)

    den = lax.fori_loop(0, size // slab, square, jnp.zeros((1, LANES), F32))
    den = jnp.where(w == 0, den, 0.0)

    shift = charge[0] - 1
    source = n - shift
    clipped = jnp.clip(source, 0, total_n - 1)
    inside = (source == clipped).astype(jnp.int32)
    rows_src, cols_src = lsizes[clipped] * inside, rsizes[clipped] * inside
    toward = shift * (1 - 2 * c)

    def along(src):
        return [push(src, src, at_x(s)) for s in range(1, NX)]

    cross.wait_recv()
    mine = far.at[h, i, :, cols(x)]
    quad_one = [push(mine, mine, at_j(h * 4 + to)) for to in quad]
    sent = [along(mine)]
    cross_four.wait_recv()
    mine = far.at[1 - h, i, :, cols(x)]
    quad_two = [push(mine, mine, at_j(h * 4 + to)) for to in quad]
    sent.append(along(mine))
    for one, two, to in zip(quad_one, quad_two, quad):
        one.wait_recv()
        two.wait_recv()
        sent.append(along(far.at[:, to, :, cols(x)]))

    def inner(xb):
        at = cols(xb)
        for t in range(NJ):
            down = pl.ds(t * tall, tall)
            took = jnp.where(
                toward == 1, far[t // 4, t % 4, :, at],
                jnp.where(toward == 0, own[down, at], near[down, at]),
            )
            took = masked(took, t * tall, xb * LANES, rows_src, cols_src)
            ph[down], plo[down] = split(took)
        ih[:, at], il[:, at] = split(product(lh[...], ll[...], ph[...], plo[...]))

    x1, x2, x3 = lax.rem(x + 1, NX), lax.rem(x + 2, NX), lax.rem(x + 3, NX)
    nearby.wait_recv()
    inner(x)
    for s, xb in ((1, x3), (3, x1), (2, x2)):
        for copies in sent:
            copies[s - 1].wait_recv()
        inner(xb)

    num = jnp.zeros((1, LANES), F32)
    for xb in (x2, x1, x3, x):
        at = rows(xb * block, block)
        t = product(ih[at], il[at], rh[...], rl[...])
        t = masked(t, xb * block, 0, rows_own, cols_own)
        term[at] = t
        num = num + lanes(t * own[at])

    g1[j] = jnp.concatenate([num, den], axis=1)
    c1 = [push(g1.at[j], g1.at[j], at_j(lax.rem(j + s, NJ))) for s in range(1, NJ)]

    u = j // 2
    places = [3 - u, u + 2 - 4 * (u // 2), u + 1 - 2 * (u % 2), u]

    def scatter(place):
        return [
            push(
                term.at[rows(xb * block + place * pair, pair)],
                from_x.at[s - 1, rows(place * pair, pair)], at_x(s),
            )
            for s, xb in ((2, x2), (1, x1), (3, x3))
        ]

    pieces = [scatter(places[0])]
    for copy in c1:
        copy.wait_recv()
    xc = x * NC + c
    s1 = g1[0]
    for t in range(1, NJ):
        s1 = s1 + g1[t]
    g2[xc] = s1
    c2 = [push(g2.at[xc], g2.at[xc], at_xc(s)) for s in range(1, NX * NC)]
    pieces.append(scatter(places[1]))
    for copy in c2:
        copy.wait_recv()
    qr = q * NR + r
    s2 = g2[0]
    for t in range(1, NX * NC):
        s2 = s2 + g2[t]
    g3[qr] = s2
    c3 = [push(g3.at[qr], g3.at[qr], at_qr(s)) for s in range(1, NQ * NR)]
    pieces.append(scatter(places[2]))
    pieces.append(scatter(places[3]))

    zs = []
    for place, copies in zip(places, pieces):
        for copy in copies:
            copy.wait_recv()
        at = rows(place * pair, pair)
        zsum[at] = (term[rows(x * block + place * pair, pair)] + from_x[0, at]) + (
            from_x[1, at] + from_x[2, at]
        )
        odd = j % 2
        two = (2 * place + odd, 2 * place + 1 - odd) if place is not u else (j + 1 - 2 * odd,)
        for other in two:
            zs.append(push(zsum.at[rows(other * band, band)], zrecv.at[j], at_j(other)))
    zrecv[j] = zsum[rows(j * band, band)]
    for copy in zs:
        copy.wait_recv()
    share = zrecv[0]
    for t in range(1, NJ):
        share = share + zrecv[t]
    mine = own[rows(w * band, band)]
    for copy in c3:
        copy.wait_recv()
    s3 = g3[0]
    for t in range(1, NQ * NR):
        s3 = s3 + g3[t]
    alpha = jnp.sum(s3[:, 0:LANES], axis=1, keepdims=True) / jnp.sum(
        s3[:, LANES:], axis=1, keepdims=True
    )
    result[0:band] = share - alpha * mine
    result[band:band + 8] = jnp.broadcast_to(alpha, (8, size))
    for copy in started:
        copy.wait_send()


def finish(result, out, alpha):
    band = out.shape[0]
    out[...] = result[0:band]
    alpha[...] = result[band:band + 1, 0:1]


def per_device(state, left_env, right_env, left_sizes, right_sizes, channel_charge):
    size = state.shape[1]
    band = size // (NX * NJ)
    block = band * NJ
    hbm = pl.BlockSpec(memory_space=pl.ANY)
    smem = pl.BlockSpec(memory_space=pltpu.SMEM)
    vmem = pl.BlockSpec(memory_space=pltpu.VMEM)
    full = (size, size)
    result = pl.pallas_call(
        kernel,
        out_shape=jax.ShapeDtypeStruct((band + 8, size), F32),
        in_specs=[hbm, hbm, hbm, smem, smem, smem],
        out_specs=vmem,
        scratch_shapes=[
            pltpu.VMEM(full, F32),
            pltpu.VMEM(full, F32),
            pltpu.VMEM(full, F32),
            pltpu.VMEM(full, F32),
            pltpu.VMEM((2, 4, size // NJ, size), F32),
            pltpu.VMEM(full, BF16),
            pltpu.VMEM(full, BF16),
            pltpu.VMEM(full, BF16),
            pltpu.VMEM(full, BF16),
            pltpu.VMEM((size, LANES), BF16),
            pltpu.VMEM((size, LANES), BF16),
            pltpu.VMEM(full, BF16),
            pltpu.VMEM(full, BF16),
            pltpu.VMEM(full, F32),
            pltpu.VMEM((NX - 1, block, size), F32),
            pltpu.VMEM((block, size), F32),
            pltpu.VMEM((NJ, band, size), F32),
            pltpu.VMEM((NJ, 1, 2 * LANES), F32),
            pltpu.VMEM((NX * NC, 1, 2 * LANES), F32),
            pltpu.VMEM((NQ * NR, 1, 2 * LANES), F32),
            pltpu.SemaphoreType.DMA((3,)),
            pltpu.SemaphoreType.DMA((COPIES,)),
            pltpu.SemaphoreType.DMA((COPIES,)),
        ],
        compiler_params=pltpu.CompilerParams(
            collective_id=0, has_side_effects=True, vmem_limit_bytes=60 << 20
        ),
    )(state[0], left_env[0, 0], right_env[0, 0], left_sizes, right_sizes, channel_charge)
    share, alpha = pl.pallas_call(
        finish,
        out_shape=(
            jax.ShapeDtypeStruct((band, size), F32),
            jax.ShapeDtypeStruct((1, 1), F32),
        ),
        in_specs=[vmem],
        out_specs=(vmem, vmem),
    )(result)
    return share[None], alpha[0, 0]


def solution(mesh):
    placed = (
        P("narrow", None, None),
        P("wide", "narrow", None, None),
        P("wide", "narrow", None, None),
        P(),
        P(),
        P("wide"),
    )
    return jax.shard_map(
        per_device,
        mesh=mesh,
        in_specs=placed,
        out_specs=(P("narrow", "wide", None), P()),
        check_vma=False,
    )
```

```python
import functools

import jax
import jax.numpy as jnp
from jax import lax
from jax.experimental import pallas as pl
from jax.experimental.pallas import tpu as pltpu
from jax.sharding import PartitionSpec as P

MESH = pl.DeviceIdType.MESH
F32 = jnp.float32
BF16 = jnp.bfloat16

NX = 4
NJ = 8
NQ = 4
NR = 4
NC = 2
LANES = 128
COPIES = 114


def split(v):
    high = v.astype(BF16)
    return high, (v - high.astype(F32)).astype(BF16)


def product(ah, al, bh, bl):
    dot = functools.partial(jnp.dot, preferred_element_type=F32)
    return dot(ah, bh) + (dot(ah, bl) + dot(al, bh))


def kernel(
    state, folded, left, right, lsizes_in, rsizes_in, charge,
    result,
    lsizes, rsizes,
    own, lenv, renv, near, far, lh, ll, rh, rl, ph, plo, ih, il, term,
    from_x, zsum, zrecv, g1, g2,
    local_sem, send_sem, recv_sem, met,
):
    size = own.shape[0]
    band = size // (NX * NJ)
    block = band * NJ
    pair = 2 * band
    tall = size // NJ
    w = lax.axis_index("wide")
    n = lax.axis_index("narrow")
    x, j = w // NJ, w % NJ
    h, i = j // 4, j % 4
    q, r, c = n // (NR * NC), (n // NC) % NR, n % NC
    total_n = NQ * NR * NC

    def at_x(step):
        return (lax.rem(x + step, NX) * NJ + j, n)

    def at_j(other):
        return (x * NJ + other, n)

    def at_xyc(step):
        to = lax.rem((x * NQ + q) * NC + c + step, NX * NQ * NC)
        return ((to // (NQ * NC)) * NJ + j, (to // NC % NQ * NR + r) * NC + to % NC)

    def at_z(step):
        to = lax.rem(r * NJ + j + step, NR * NJ)
        return (x * NJ + to % NJ, (q * NR + to // NJ) * NC + c)

    def at_run(step, core):
        return (w, (q * NR + lax.rem(r + step, NR)) * NC + core)

    sibling = (w, n + 1 - 2 * c)
    across = (w, lax.rem(n + 2 * c - 1 + total_n, total_n))
    quad = [i + 1 - 2 * (i % 2), i + 2 - 4 * (i // 2), 3 - i]

    own_copy = pltpu.make_async_copy(state, own, local_sem.at[0])
    left_copy = pltpu.make_async_copy(left, lenv, local_sem.at[1])
    right_copy = pltpu.make_async_copy(right, renv, local_sem.at[2])

    small = [
        pltpu.make_async_copy(src, dst, local_sem.at[3 + t])
        for t, (src, dst) in enumerate(
            ((lsizes_in, lsizes), (rsizes_in, rsizes))
        )
    ]

    barrier = pltpu.get_barrier_semaphore()
    partners = (
        [across]
        + [at_run(s, core) for s in (1, NR - 1) for core in range(NC)]
        + [at_j(lax.rem(j + s, NJ)) for s in range(1, NJ)]
        + [at_xyc(s) for s in range(1, NX * NQ * NC)]
    )
    for partner in partners:
        pl.semaphore_signal(barrier, inc=1, device_id=partner, device_id_type=MESH)
    right_copy.start()
    own_copy.start()
    left_copy.start()
    for copy in small:
        copy.start()
    pl.semaphore_wait(barrier, len(partners))

    started = []

    def push(src, dst, device):
        i = len(started)
        copy = pltpu.make_async_remote_copy(
            src_ref=src, dst_ref=dst, send_sem=send_sem.at[i], recv_sem=recv_sem.at[i],
            device_id=device, device_id_type=MESH,
        )
        copy.start()
        started.append(copy)
        return copy

    def rows(start, count):
        return pl.ds(pl.multiple_of(start, 8), count)

    def cols(xb):
        return pl.ds(pl.multiple_of(xb * LANES, LANES), LANES)

    def bands(ref, k, t):
        return ref.at[:, k, rows(t * (tall // 2), tall // 2), cols(x)]

    cross = [push(bands(folded, i, t), bands(far, i, t), across) for t in range(2)]
    nearby = push(state, near, sibling)

    slab = 32
    right_copy.wait()
    for t in range(size // LANES):
        at = pl.ds(t * LANES, LANES)
        rh[at, :], rl[at, :] = split(renv[:, at].T)

    left_copy.wait()

    @pl.loop(0, size // slab)
    def _(t):
        at = rows(t * slab, slab)
        lh[at], ll[at] = split(lenv[at])

    own_copy.wait()
    for copy in small:
        copy.wait()
    rows_own, cols_own = lsizes[n], rsizes[n]

    def masked(values, first, across_first, rlimit, climit):
        rid = lax.broadcasted_iota(jnp.int32, values.shape, 0) + first
        cid = lax.broadcasted_iota(jnp.int32, values.shape, 1) + across_first
        return jnp.where((rid < rlimit) & (cid < climit), values, 0.0)

    def lanes(values):
        s = jnp.sum(values, axis=0, keepdims=True)
        return s[:, 0:128] + s[:, 128:256] + s[:, 256:384] + s[:, 384:512]

    def square(t, total):
        at = rows(t * slab, slab)
        psi = masked(own[at], t * slab, 0, rows_own, cols_own)
        own[at] = psi
        return total + lanes(psi * psi)

    den = lax.fori_loop(0, size // slab, square, jnp.zeros((1, LANES), F32))
    den = jnp.where(w == 0, den, 0.0)

    shift = charge[0] - 1
    source = n - shift
    clipped = jnp.clip(source, 0, total_n - 1)
    inside = (source == clipped).astype(jnp.int32)
    rows_src, cols_src = lsizes[clipped] * inside, rsizes[clipped] * inside
    toward = shift * (1 - 2 * c)

    def along(src):
        return [push(src, src, at_x(s)) for s in range(1, NX)]

    quads, sent = [], []
    for t in range(2):
        cross[t].wait_recv()
        mine = bands(far, i, t)
        quads.append([push(mine, mine, at_j(h * 4 + to)) for to in quad])
        sent.append(along(mine))
    for t in range(2):
        for copy, to in zip(quads[t], quad):
            copy.wait_recv()
            sent.append(along(bands(far, to, t)))
    pl.semaphore_signal(met, inc=1, device_id=at_j((1 - h) * 4 + i), device_id_type=MESH)

    def inner(xb):
        at = cols(xb)
        for t in range(NJ):
            down = pl.ds(t * tall, tall)
            took = jnp.where(
                toward == 1, far[t // 4, t % 4, :, at],
                jnp.where(toward == 0, own[down, at], near[down, at]),
            )
            took = masked(took, t * tall, xb * LANES, rows_src, cols_src)
            ph[down], plo[down] = split(took)
        ih[:, at], il[:, at] = split(product(lh[...], ll[...], ph[...], plo[...]))

    x1, x2, x3 = lax.rem(x + 1, NX), lax.rem(x + 2, NX), lax.rem(x + 3, NX)
    nearby.wait_recv()
    inner(x)
    for s, xb in ((1, x3), (3, x1), (2, x2)):
        for copies in sent:
            copies[s - 1].wait_recv()
        inner(xb)

    num = jnp.zeros((1, LANES), F32)
    for xb in (x2, x1, x3, x):
        at = rows(xb * block, block)
        t = product(ih[at], il[at], rh[...], rl[...])
        t = masked(t, xb * block, 0, rows_own, cols_own)
        term[at] = t
        num = num + lanes(t * own[at])

    pl.semaphore_wait(met, 1)
    xyc = (x * NQ + q) * NC + c
    g1[xyc] = jnp.concatenate([num, den], axis=1)
    c1 = [push(g1.at[xyc], g1.at[xyc], at_xyc(s)) for s in range(1, NX * NQ * NC)]

    u = j // 2
    places = [3 - u, u + 2 - 4 * (u // 2), u + 1 - 2 * (u % 2), u]

    def scatter(place):
        return [
            push(
                term.at[rows(xb * block + place * pair, pair)],
                from_x.at[s - 1, rows(place * pair, pair)], at_x(s),
            )
            for s, xb in ((2, x2), (1, x1), (3, x3))
        ]

    pieces = [scatter(place) for place in places[:2]]
    for copy in c1:
        copy.wait_recv()
    zz = r * NJ + j
    s1 = g1[0]
    for t in range(1, NX * NQ * NC):
        s1 = s1 + g1[t]
    g2[zz] = s1
    farthest_first = sorted(range(1, NR * NJ), key=lambda s: -min(s, NR * NJ - s))
    c2 = [push(g2.at[zz], g2.at[zz], at_z(s)) for s in farthest_first]
    pieces += [scatter(place) for place in places[2:]]

    zs = []
    for place, copies in zip(places, pieces):
        for copy in copies:
            copy.wait_recv()
        at = rows(place * pair, pair)
        zsum[at] = (term[rows(x * block + place * pair, pair)] + from_x[0, at]) + (
            from_x[1, at] + from_x[2, at]
        )
        odd = j % 2
        two = (2 * place + odd, 2 * place + 1 - odd) if place is not u else (j + 1 - 2 * odd,)
        for other in two:
            zs.append(push(zsum.at[rows(other * band, band)], zrecv.at[j], at_j(other)))
    zrecv[j] = zsum[rows(j * band, band)]
    for copy in zs:
        copy.wait_recv()
    share = zrecv[0]
    for t in range(1, NJ):
        share = share + zrecv[t]
    mine = own[rows(w * band, band)]
    for copy in c2:
        copy.wait_recv()
    s2 = g2[0]
    for t in range(1, NR * NJ):
        s2 = s2 + g2[t]
    alpha = jnp.sum(s2[:, 0:LANES], axis=1, keepdims=True) / jnp.sum(
        s2[:, LANES:], axis=1, keepdims=True
    )
    result[0:band] = share - alpha * mine
    result[band:band + 8] = jnp.broadcast_to(alpha, (8, size))
    for copy in started:
        copy.wait_send()


def finish(result, out, alpha):
    band = out.shape[0]
    out[...] = result[0:band]
    alpha[...] = result[band:band + 1, 0:1]


def per_device(state, left_env, right_env, left_sizes, right_sizes, channel_charge):
    size = state.shape[1]
    band = size // (NX * NJ)
    block = band * NJ
    hbm = pl.BlockSpec(memory_space=pl.ANY)
    vmem = pl.BlockSpec(memory_space=pltpu.VMEM)
    full = (size, size)
    result = pl.pallas_call(
        kernel,
        out_shape=jax.ShapeDtypeStruct((band + 8, size), F32),
        in_specs=[hbm] * 6 + [pl.BlockSpec(memory_space=pltpu.SMEM)],
        out_specs=vmem,
        scratch_shapes=[
            pltpu.SMEM(left_sizes.shape, jnp.int32),
            pltpu.SMEM(right_sizes.shape, jnp.int32),
            pltpu.VMEM(full, F32),
            pltpu.VMEM(full, F32),
            pltpu.VMEM(full, F32),
            pltpu.VMEM(full, F32),
            pltpu.VMEM((2, 4, size // NJ, size), F32),
            pltpu.VMEM(full, BF16),
            pltpu.VMEM(full, BF16),
            pltpu.VMEM(full, BF16),
            pltpu.VMEM(full, BF16),
            pltpu.VMEM((size, LANES), BF16),
            pltpu.VMEM((size, LANES), BF16),
            pltpu.VMEM(full, BF16),
            pltpu.VMEM(full, BF16),
            pltpu.VMEM(full, F32),
            pltpu.VMEM((NX - 1, block, size), F32),
            pltpu.VMEM((block, size), F32),
            pltpu.VMEM((NJ, band, size), F32),
            pltpu.VMEM((NX * NQ * NC, 1, 2 * LANES), F32),
            pltpu.VMEM((NR * NJ, 1, 2 * LANES), F32),
            pltpu.SemaphoreType.DMA((5,)),
            pltpu.SemaphoreType.DMA((COPIES,)),
            pltpu.SemaphoreType.DMA((COPIES,)),
            pltpu.SemaphoreType.REGULAR,
        ],
        compiler_params=pltpu.CompilerParams(
            collective_id=0, has_side_effects=True, vmem_limit_bytes=60 << 20
        ),
    )(state[0], state[0].reshape(2, 4, size // NJ, size), left_env[0, 0], right_env[0, 0], left_sizes, right_sizes, channel_charge)
    share, alpha = pl.pallas_call(
        finish,
        out_shape=(
            jax.ShapeDtypeStruct((band, size), F32),
            jax.ShapeDtypeStruct((1, 1), F32),
        ),
        in_specs=[vmem],
        out_specs=(vmem, vmem),
    )(result)
    return share[None], alpha[0, 0]


def solution(mesh):
    placed = (
        P("narrow", None, None),
        P("wide", "narrow", None, None),
        P("wide", "narrow", None, None),
        P(),
        P(),
        P("wide"),
    )
    return jax.shard_map(
        per_device,
        mesh=mesh,
        in_specs=placed,
        out_specs=(P("narrow", "wide", None), P()),
        check_vma=False,
    )
```

```python
import functools

import jax
import jax.numpy as jnp
from jax import lax
from jax.experimental import pallas as pl
from jax.experimental.pallas import tpu as pltpu
from jax.sharding import PartitionSpec as P

MESH = pl.DeviceIdType.MESH
F32 = jnp.float32
BF16 = jnp.bfloat16

NX = 4
NJ = 8
NQ = 4
NR = 4
NC = 2
LANES = 128
COPIES = 114


def split(v):
    high = v.astype(BF16)
    return high, (v - high.astype(F32)).astype(BF16)


def product(ah, al, bh, bl):
    dot = functools.partial(jnp.dot, preferred_element_type=F32)
    return dot(ah, bh) + (dot(ah, bl) + dot(al, bh))


def kernel(
    state, folded, left, right, lsizes_in, rsizes_in, charge,
    result,
    lsizes, rsizes,
    own, lenv, renv, near, far, lh, ll, rh, rl, ph, plo, ih, il, term,
    from_x, zsum, zrecv, g1, g2,
    local_sem, send_sem, recv_sem, met, told,
):
    size = own.shape[0]
    band = size // (NX * NJ)
    block = band * NJ
    pair = 2 * band
    tall = size // NJ
    w = lax.axis_index("wide")
    n = lax.axis_index("narrow")
    x, j = w // NJ, w % NJ
    h, i = j // 4, j % 4
    q, r, c = n // (NR * NC), (n // NC) % NR, n % NC
    total_n = NQ * NR * NC

    def at_x(step):
        return (lax.rem(x + step, NX) * NJ + j, n)

    def at_j(other):
        return (x * NJ + other, n)

    def at_xyc(step):
        to = lax.rem((x * NQ + q) * NC + c + step, NX * NQ * NC)
        return ((to // (NQ * NC)) * NJ + j, (to // NC % NQ * NR + r) * NC + to % NC)

    def at_z(step):
        to = lax.rem(r * NJ + j + step, NR * NJ)
        return (x * NJ + to % NJ, (q * NR + to // NJ) * NC + c)

    def at_y(step, core):
        return (w, (lax.rem(q + step, NQ) * NR + r) * NC + core)

    def at_run(step, core):
        return (w, (q * NR + lax.rem(r + step, NR)) * NC + core)

    sibling = (w, n + 1 - 2 * c)
    across = (w, lax.rem(n + 2 * c - 1 + total_n, total_n))
    quad = [i + 1 - 2 * (i % 2), i + 2 - 4 * (i // 2), 3 - i]

    own_copy = pltpu.make_async_copy(state, own, local_sem.at[0])
    left_copy = pltpu.make_async_copy(left, lenv, local_sem.at[1])
    right_copy = pltpu.make_async_copy(right, renv, local_sem.at[2])

    small = [
        pltpu.make_async_copy(src, dst, local_sem.at[3 + t])
        for t, (src, dst) in enumerate(
            ((lsizes_in, lsizes), (rsizes_in, rsizes))
        )
    ]

    barrier = pltpu.get_barrier_semaphore()
    partners = (
        [across]
        + [at_run(s, core) for s in (1, NR - 1) for core in range(NC)]
        + [at_j(lax.rem(j + s, NJ)) for s in range(1, NJ)]
        + [at_xyc(s) for s in range(1, NX * NQ * NC)]
    )
    for partner in partners:
        pl.semaphore_signal(barrier, inc=1, device_id=partner, device_id_type=MESH)
    right_copy.start()
    own_copy.start()
    left_copy.start()
    for copy in small:
        copy.start()
    pl.semaphore_wait(barrier, len(partners))

    started = []

    def push(src, dst, device):
        i = len(started)
        copy = pltpu.make_async_remote_copy(
            src_ref=src, dst_ref=dst, send_sem=send_sem.at[i], recv_sem=recv_sem.at[i],
            device_id=device, device_id_type=MESH,
        )
        copy.start()
        started.append(copy)
        return copy

    def rows(start, count):
        return pl.ds(pl.multiple_of(start, 8), count)

    def cols(xb):
        return pl.ds(pl.multiple_of(xb * LANES, LANES), LANES)

    def bands(ref, k, t):
        return ref.at[:, k, rows(t * (tall // 2), tall // 2), cols(x)]

    cross = [push(bands(folded, i, t), bands(far, i, t), across) for t in range(2)]
    nearby = push(state, near, sibling)

    slab = 32
    right_copy.wait()
    for t in range(size // LANES):
        at = pl.ds(t * LANES, LANES)
        rh[at, :], rl[at, :] = split(renv[:, at].T)

    left_copy.wait()

    @pl.loop(0, size // slab)
    def _(t):
        at = rows(t * slab, slab)
        lh[at], ll[at] = split(lenv[at])

    own_copy.wait()
    for copy in small:
        copy.wait()
    rows_own, cols_own = lsizes[n], rsizes[n]

    def masked(values, first, across_first, rlimit, climit):
        rid = lax.broadcasted_iota(jnp.int32, values.shape, 0) + first
        cid = lax.broadcasted_iota(jnp.int32, values.shape, 1) + across_first
        return jnp.where((rid < rlimit) & (cid < climit), values, 0.0)

    def lanes(values):
        s = jnp.sum(values, axis=0, keepdims=True)
        return s[:, 0:128] + s[:, 128:256] + s[:, 256:384] + s[:, 384:512]

    def square(t, total):
        at = rows(t * slab, slab)
        psi = masked(own[at], t * slab, 0, rows_own, cols_own)
        own[at] = psi
        return total + lanes(psi * psi)

    den = lax.fori_loop(0, size // slab, square, jnp.zeros((1, LANES), F32))
    den = jnp.where(w == 0, den, 0.0)

    shift = charge[0] - 1
    source = n - shift
    clipped = jnp.clip(source, 0, total_n - 1)
    inside = (source == clipped).astype(jnp.int32)
    rows_src, cols_src = lsizes[clipped] * inside, rsizes[clipped] * inside
    toward = shift * (1 - 2 * c)

    def along(src):
        return [push(src, src, at_x(s)) for s in range(1, NX)]

    quads, sent = [], []
    for t in range(2):
        cross[t].wait_recv()
        mine = bands(far, i, t)
        quads.append([push(mine, mine, at_j(h * 4 + to)) for to in quad])
        sent.append(along(mine))
    for t in range(2):
        for copy, to in zip(quads[t], quad):
            copy.wait_recv()
            sent.append(along(bands(far, to, t)))
    pl.semaphore_signal(met, inc=1, device_id=at_j((1 - h) * 4 + i), device_id_type=MESH)

    def inner(xb):
        at = cols(xb)
        for t in range(NJ):
            down = pl.ds(t * tall, tall)
            took = jnp.where(
                toward == 1, far[t // 4, t % 4, :, at],
                jnp.where(toward == 0, own[down, at], near[down, at]),
            )
            took = masked(took, t * tall, xb * LANES, rows_src, cols_src)
            ph[down], plo[down] = split(took)
        ih[:, at], il[:, at] = split(product(lh[...], ll[...], ph[...], plo[...]))

    x1, x2, x3 = lax.rem(x + 1, NX), lax.rem(x + 2, NX), lax.rem(x + 3, NX)
    nearby.wait_recv()
    inner(x)
    pl.semaphore_wait(met, 1)
    tell = [sibling] + [at_y(s, core) for s in (1, NQ - 1) for core in range(NC)]
    for partner in tell:
        pl.semaphore_signal(told, inc=1, device_id=partner, device_id_type=MESH)
    for s, xb in ((1, x3), (3, x1), (2, x2)):
        for copies in sent:
            copies[s - 1].wait_recv()
        inner(xb)

    num = jnp.zeros((1, LANES), F32)
    for xb in (x2, x1, x3, x):
        at = rows(xb * block, block)
        t = product(ih[at], il[at], rh[...], rl[...])
        t = masked(t, xb * block, 0, rows_own, cols_own)
        term[at] = t
        num = num + lanes(t * own[at])

    pl.semaphore_wait(told, len(tell))
    zz = r * NJ + j
    g2[zz] = jnp.concatenate([num, den], axis=1)
    farthest_first = sorted(range(1, NR * NJ), key=lambda s: -min(s, NR * NJ - s))
    c1 = [push(g2.at[zz], g2.at[zz], at_z(s)) for s in farthest_first]

    u = j // 2
    places = [3 - u, u + 2 - 4 * (u // 2), u + 1 - 2 * (u % 2), u]

    def scatter(place):
        return [
            push(
                term.at[rows(xb * block + place * pair, pair)],
                from_x.at[s - 1, rows(place * pair, pair)], at_x(s),
            )
            for s, xb in ((2, x2), (1, x1), (3, x3))
        ]

    pieces = [scatter(place) for place in places]
    zs = []

    def along_z(some):
        for place, copies in zip(places[some], pieces[some]):
            for copy in copies:
                copy.wait_recv()
            at = rows(place * pair, pair)
            zsum[at] = (term[rows(x * block + place * pair, pair)] + from_x[0, at]) + (
                from_x[1, at] + from_x[2, at]
            )
            odd = j % 2
            two = (2 * place + odd, 2 * place + 1 - odd) if place is not u else (j + 1 - 2 * odd,)
            for other in two:
                zs.append(push(zsum.at[rows(other * band, band)], zrecv.at[j], at_j(other)))

    along_z(slice(0, 3))
    for copy in c1:
        copy.wait_recv()
    xyc = (x * NQ + q) * NC + c
    s1 = g2[0]
    for t in range(1, NR * NJ):
        s1 = s1 + g2[t]
    g1[xyc] = s1
    c2 = [push(g1.at[xyc], g1.at[xyc], at_xyc(s)) for s in range(1, NX * NQ * NC)]
    along_z(slice(3, 4))
    zrecv[j] = zsum[rows(j * band, band)]
    for copy in zs:
        copy.wait_recv()
    share = zrecv[0]
    for t in range(1, NJ):
        share = share + zrecv[t]
    mine = own[rows(w * band, band)]
    for copy in c2:
        copy.wait_recv()
    s2 = g1[0]
    for t in range(1, NX * NQ * NC):
        s2 = s2 + g1[t]
    alpha = jnp.sum(s2[:, 0:LANES], axis=1, keepdims=True) / jnp.sum(
        s2[:, LANES:], axis=1, keepdims=True
    )
    result[0:band] = share - alpha * mine
    result[band:band + 8] = jnp.broadcast_to(alpha, (8, size))
    for copy in started:
        copy.wait_send()


def finish(result, out, alpha):
    band = out.shape[0]
    out[...] = result[0:band]
    alpha[...] = result[band:band + 1, 0:1]


def per_device(state, left_env, right_env, left_sizes, right_sizes, channel_charge):
    size = state.shape[1]
    band = size // (NX * NJ)
    block = band * NJ
    hbm = pl.BlockSpec(memory_space=pl.ANY)
    vmem = pl.BlockSpec(memory_space=pltpu.VMEM)
    full = (size, size)
    result = pl.pallas_call(
        kernel,
        out_shape=jax.ShapeDtypeStruct((band + 8, size), F32),
        in_specs=[hbm] * 6 + [pl.BlockSpec(memory_space=pltpu.SMEM)],
        out_specs=vmem,
        scratch_shapes=[
            pltpu.SMEM(left_sizes.shape, jnp.int32),
            pltpu.SMEM(right_sizes.shape, jnp.int32),
            pltpu.VMEM(full, F32),
            pltpu.VMEM(full, F32),
            pltpu.VMEM(full, F32),
            pltpu.VMEM(full, F32),
            pltpu.VMEM((2, 4, size // NJ, size), F32),
            pltpu.VMEM(full, BF16),
            pltpu.VMEM(full, BF16),
            pltpu.VMEM(full, BF16),
            pltpu.VMEM(full, BF16),
            pltpu.VMEM((size, LANES), BF16),
            pltpu.VMEM((size, LANES), BF16),
            pltpu.VMEM(full, BF16),
            pltpu.VMEM(full, BF16),
            pltpu.VMEM(full, F32),
            pltpu.VMEM((NX - 1, block, size), F32),
            pltpu.VMEM((block, size), F32),
            pltpu.VMEM((NJ, band, size), F32),
            pltpu.VMEM((NX * NQ * NC, 1, 2 * LANES), F32),
            pltpu.VMEM((NR * NJ, 1, 2 * LANES), F32),
            pltpu.SemaphoreType.DMA((5,)),
            pltpu.SemaphoreType.DMA((COPIES,)),
            pltpu.SemaphoreType.DMA((COPIES,)),
            pltpu.SemaphoreType.REGULAR,
            pltpu.SemaphoreType.REGULAR,
        ],
        compiler_params=pltpu.CompilerParams(
            collective_id=0, has_side_effects=True, vmem_limit_bytes=60 << 20
        ),
    )(state[0], state[0].reshape(2, 4, size // NJ, size), left_env[0, 0], right_env[0, 0], left_sizes, right_sizes, channel_charge)
    share, alpha = pl.pallas_call(
        finish,
        out_shape=(
            jax.ShapeDtypeStruct((band, size), F32),
            jax.ShapeDtypeStruct((1, 1), F32),
        ),
        in_specs=[vmem],
        out_specs=(vmem, vmem),
    )(result)
    return share[None], alpha[0, 0]


def solution(mesh):
    placed = (
        P("narrow", None, None),
        P("wide", "narrow", None, None),
        P("wide", "narrow", None, None),
        P(),
        P(),
        P("wide"),
    )
    return jax.shard_map(
        per_device,
        mesh=mesh,
        in_specs=placed,
        out_specs=(P("narrow", "wide", None), P()),
        check_vma=False,
    )
```

```python
import functools

import jax
import jax.numpy as jnp
from jax import lax
from jax.experimental import pallas as pl
from jax.experimental.pallas import tpu as pltpu
from jax.sharding import PartitionSpec as P

MESH = pl.DeviceIdType.MESH
F32 = jnp.float32
BF16 = jnp.bfloat16

NX = 4
NJ = 8
NQ = 4
NR = 4
NC = 2
LANES = 128
COPIES = 119


def split(v):
    high = v.astype(BF16)
    return high, (v - high.astype(F32)).astype(BF16)


def product(ah, al, bh, bl):
    dot = functools.partial(jnp.dot, preferred_element_type=F32)
    return dot(ah, bh) + (dot(ah, bl) + dot(al, bh))


def kernel(
    state, folded, left, right, lsizes_in, rsizes_in, charge,
    result,
    lsizes, rsizes,
    own, lenv, renv, near, far, lh, ll, rh, rl, ph, plo, ih, il, term,
    from_x, zsum, zrecv, g1, g2,
    local_sem, send_sem, recv_sem, met, told,
):
    size = own.shape[0]
    band = size // (NX * NJ)
    block = band * NJ
    pair = 2 * band
    tall = size // NJ
    w = lax.axis_index("wide")
    n = lax.axis_index("narrow")
    x, j = w // NJ, w % NJ
    h, i = j // 4, j % 4
    q, r, c = n // (NR * NC), (n // NC) % NR, n % NC
    total_n = NQ * NR * NC

    def at_x(step):
        return (lax.rem(x + step, NX) * NJ + j, n)

    def at_j(other):
        return (x * NJ + other, n)

    def at_xyc(step):
        to = lax.rem((x * NQ + q) * NC + c + step, NX * NQ * NC)
        return ((to // (NQ * NC)) * NJ + j, (to // NC % NQ * NR + r) * NC + to % NC)

    def at_z(step):
        to = lax.rem(r * NJ + j + step, NR * NJ)
        return (x * NJ + to % NJ, (q * NR + to // NJ) * NC + c)

    def at_y(step, core):
        return (w, (lax.rem(q + step, NQ) * NR + r) * NC + core)

    def at_run(step, core):
        return (w, (q * NR + lax.rem(r + step, NR)) * NC + core)

    sibling = (w, n + 1 - 2 * c)
    across = (w, lax.rem(n + 2 * c - 1 + total_n, total_n))
    quad = [i + 1 - 2 * (i % 2), i + 2 - 4 * (i // 2), 3 - i]

    own_copy = pltpu.make_async_copy(state, own, local_sem.at[0])
    left_copy = pltpu.make_async_copy(left, lenv, local_sem.at[1])
    right_copy = pltpu.make_async_copy(right, renv, local_sem.at[2])

    small = [
        pltpu.make_async_copy(src, dst, local_sem.at[3 + t])
        for t, (src, dst) in enumerate(
            ((lsizes_in, lsizes), (rsizes_in, rsizes))
        )
    ]

    barrier = pltpu.get_barrier_semaphore()
    partners = (
        [across]
        + [at_run(s, core) for s in (1, NR - 1) for core in range(NC)]
        + [at_j(lax.rem(j + s, NJ)) for s in range(1, NJ)]
        + [at_xyc(s) for s in range(1, NX * NQ * NC)]
    )
    for partner in partners:
        pl.semaphore_signal(barrier, inc=1, device_id=partner, device_id_type=MESH)
    right_copy.start()
    own_copy.start()
    left_copy.start()
    for copy in small:
        copy.start()
    pl.semaphore_wait(barrier, len(partners))

    started = []

    def push(src, dst, device):
        i = len(started)
        copy = pltpu.make_async_remote_copy(
            src_ref=src, dst_ref=dst, send_sem=send_sem.at[i], recv_sem=recv_sem.at[i],
            device_id=device, device_id_type=MESH,
        )
        copy.start()
        started.append(copy)
        return copy

    def rows(start, count):
        return pl.ds(pl.multiple_of(start, 8), count)

    def cols(xb):
        return pl.ds(pl.multiple_of(xb * LANES, LANES), LANES)

    def bands(ref, k, t):
        return ref.at[:, k, rows(t * (tall // 2), tall // 2), cols(x)]

    cross = [push(bands(folded, i, t), bands(far, i, t), across) for t in range(2)]
    nearby = push(state, near, sibling)

    slab = 32
    right_copy.wait()
    for t in range(size // LANES):
        at = pl.ds(t * LANES, LANES)
        rh[at, :], rl[at, :] = split(renv[:, at].T)

    left_copy.wait()

    @pl.loop(0, size // slab)
    def _(t):
        at = rows(t * slab, slab)
        lh[at], ll[at] = split(lenv[at])

    own_copy.wait()
    for copy in small:
        copy.wait()
    rows_own, cols_own = lsizes[n], rsizes[n]

    def masked(values, first, across_first, rlimit, climit):
        rid = lax.broadcasted_iota(jnp.int32, values.shape, 0) + first
        cid = lax.broadcasted_iota(jnp.int32, values.shape, 1) + across_first
        return jnp.where((rid < rlimit) & (cid < climit), values, 0.0)

    def lanes(values):
        s = jnp.sum(values, axis=0, keepdims=True)
        return s[:, 0:128] + s[:, 128:256] + s[:, 256:384] + s[:, 384:512]

    def square(t, total):
        at = rows(t * slab, slab)
        psi = masked(own[at], t * slab, 0, rows_own, cols_own)
        own[at] = psi
        return total + lanes(psi * psi)

    den = lax.fori_loop(0, size // slab, square, jnp.zeros((1, LANES), F32))
    den = jnp.where(w == 0, den, 0.0)

    shift = charge[0] - 1
    source = n - shift
    clipped = jnp.clip(source, 0, total_n - 1)
    inside = (source == clipped).astype(jnp.int32)
    rows_src, cols_src = lsizes[clipped] * inside, rsizes[clipped] * inside
    toward = shift * (1 - 2 * c)

    def along(src):
        return [push(src, src, at_x(s)) for s in (1, 3, 2)]

    def beside(src):
        return [push(src, src, at_x(s)) for s in (1, 3)]

    def band_of(side, k, t, xb):
        return far.at[side, k, rows(t * (tall // 2), tall // 2), cols(xb)]

    def relay(k, t, copies):
        copies[0].wait_recv()
        onward = band_of(0, k, t, x3)
        copies.append(push(onward, onward, at_x(1)))
        copies[1].wait_recv()
        onward = band_of(1, k, t, x1)
        copies.append(push(onward, onward, at_x(3)))

    x1, x2, x3 = lax.rem(x + 1, NX), lax.rem(x + 2, NX), lax.rem(x + 3, NX)
    quads, early, late = [], [], []
    for t in range(2):
        cross[t].wait_recv()
        mine = bands(far, i, t)
        quads.append([push(mine, mine, at_j(h * 4 + to)) for to in quad])
        early.append((i, t, beside(mine)))
    for copy, to in zip(quads[0], quad):
        copy.wait_recv()
        early.append((to, 0, beside(bands(far, to, 0))))
    for piece in early[:2]:
        relay(*piece)
    for copy, to in zip(quads[1], quad):
        copy.wait_recv()
        late.append(along(bands(far, to, 1)))
    pl.semaphore_signal(met, inc=1, device_id=at_j((1 - h) * 4 + i), device_id_type=MESH)
    for piece in early[2:]:
        relay(*piece)

    def inner(xb):
        at = cols(xb)
        for t in range(NJ):
            down = pl.ds(t * tall, tall)
            took = jnp.where(
                toward == 1, far[t // 4, t % 4, :, at],
                jnp.where(toward == 0, own[down, at], near[down, at]),
            )
            took = masked(took, t * tall, xb * LANES, rows_src, cols_src)
            ph[down], plo[down] = split(took)
        ih[:, at], il[:, at] = split(product(lh[...], ll[...], ph[...], plo[...]))

    nearby.wait_recv()
    inner(x)
    pl.semaphore_wait(met, 1)
    tell = [sibling] + [at_y(s, core) for s in (1, NQ - 1) for core in range(NC)]
    for partner in tell:
        pl.semaphore_signal(told, inc=1, device_id=partner, device_id_type=MESH)
    for place, xb in enumerate((x3, x1, x2)):
        for copies in late:
            copies[place].wait_recv()
        if xb is x2:
            for _, _, copies in early:
                copies[2].wait_recv()
                copies[3].wait_recv()
        inner(xb)

    num = jnp.zeros((1, LANES), F32)
    for xb in (x2, x1, x3, x):
        at = rows(xb * block, block)
        t = product(ih[at], il[at], rh[...], rl[...])
        t = masked(t, xb * block, 0, rows_own, cols_own)
        term[at] = t
        num = num + lanes(t * own[at])

    pl.semaphore_wait(told, len(tell))
    zz = r * NJ + j
    g2[zz] = jnp.concatenate([num, den], axis=1)
    farthest_first = sorted(range(1, NR * NJ), key=lambda s: -min(s, NR * NJ - s))
    c1 = [push(g2.at[zz], g2.at[zz], at_z(s)) for s in farthest_first]

    u = j // 2
    places = [3 - u, u + 2 - 4 * (u // 2), u + 1 - 2 * (u % 2), u]

    def scatter(place):
        return [
            push(
                term.at[rows(xb * block + place * pair, pair)],
                from_x.at[s - 1, rows(place * pair, pair)], at_x(s),
            )
            for s, xb in ((2, x2), (1, x1), (3, x3))
        ]

    pieces = [scatter(place) for place in places]
    zs = []

    def along_z(some):
        for place, copies in zip(places[some], pieces[some]):
            for copy in copies:
                copy.wait_recv()
            at = rows(place * pair, pair)
            zsum[at] = (term[rows(x * block + place * pair, pair)] + from_x[0, at]) + (
                from_x[1, at] + from_x[2, at]
            )
            odd = j % 2
            two = (2 * place + odd, 2 * place + 1 - odd) if place is not u else (j + 1 - 2 * odd,)
            for other in two:
                zs.append(push(zsum.at[rows(other * band, band)], zrecv.at[j], at_j(other)))

    along_z(slice(0, 3))
    for copy in c1:
        copy.wait_recv()
    xyc = (x * NQ + q) * NC + c
    s1 = g2[0]
    for t in range(1, NR * NJ):
        s1 = s1 + g2[t]
    g1[xyc] = s1
    c2 = [push(g1.at[xyc], g1.at[xyc], at_xyc(s)) for s in range(1, NX * NQ * NC)]
    along_z(slice(3, 4))
    zrecv[j] = zsum[rows(j * band, band)]
    for copy in zs:
        copy.wait_recv()
    share = zrecv[0]
    for t in range(1, NJ):
        share = share + zrecv[t]
    mine = own[rows(w * band, band)]
    for copy in c2:
        copy.wait_recv()
    s2 = g1[0]
    for t in range(1, NX * NQ * NC):
        s2 = s2 + g1[t]
    alpha = jnp.sum(s2[:, 0:LANES], axis=1, keepdims=True) / jnp.sum(
        s2[:, LANES:], axis=1, keepdims=True
    )
    result[0:band] = share - alpha * mine
    result[band:band + 8] = jnp.broadcast_to(alpha, (8, size))
    for copy in started:
        copy.wait_send()


def finish(result, out, alpha):
    band = out.shape[0]
    out[...] = result[0:band]
    alpha[...] = result[band:band + 1, 0:1]


def per_device(state, left_env, right_env, left_sizes, right_sizes, channel_charge):
    size = state.shape[1]
    band = size // (NX * NJ)
    block = band * NJ
    hbm = pl.BlockSpec(memory_space=pl.ANY)
    vmem = pl.BlockSpec(memory_space=pltpu.VMEM)
    full = (size, size)
    result = pl.pallas_call(
        kernel,
        out_shape=jax.ShapeDtypeStruct((band + 8, size), F32),
        in_specs=[hbm] * 6 + [pl.BlockSpec(memory_space=pltpu.SMEM)],
        out_specs=vmem,
        scratch_shapes=[
            pltpu.SMEM(left_sizes.shape, jnp.int32),
            pltpu.SMEM(right_sizes.shape, jnp.int32),
            pltpu.VMEM(full, F32),
            pltpu.VMEM(full, F32),
            pltpu.VMEM(full, F32),
            pltpu.VMEM(full, F32),
            pltpu.VMEM((2, 4, size // NJ, size), F32),
            pltpu.VMEM(full, BF16),
            pltpu.VMEM(full, BF16),
            pltpu.VMEM(full, BF16),
            pltpu.VMEM(full, BF16),
            pltpu.VMEM((size, LANES), BF16),
            pltpu.VMEM((size, LANES), BF16),
            pltpu.VMEM(full, BF16),
            pltpu.VMEM(full, BF16),
            pltpu.VMEM(full, F32),
            pltpu.VMEM((NX - 1, block, size), F32),
            pltpu.VMEM((block, size), F32),
            pltpu.VMEM((NJ, band, size), F32),
            pltpu.VMEM((NX * NQ * NC, 1, 2 * LANES), F32),
            pltpu.VMEM((NR * NJ, 1, 2 * LANES), F32),
            pltpu.SemaphoreType.DMA((5,)),
            pltpu.SemaphoreType.DMA((COPIES,)),
            pltpu.SemaphoreType.DMA((COPIES,)),
            pltpu.SemaphoreType.REGULAR,
            pltpu.SemaphoreType.REGULAR,
        ],
        compiler_params=pltpu.CompilerParams(
            collective_id=0, has_side_effects=True, vmem_limit_bytes=60 << 20
        ),
    )(state[0], state[0].reshape(2, 4, size // NJ, size), left_env[0, 0], right_env[0, 0], left_sizes, right_sizes, channel_charge)
    share, alpha = pl.pallas_call(
        finish,
        out_shape=(
            jax.ShapeDtypeStruct((band, size), F32),
            jax.ShapeDtypeStruct((1, 1), F32),
        ),
        in_specs=[vmem],
        out_specs=(vmem, vmem),
    )(result)
    return share[None], alpha[0, 0]


def solution(mesh):
    placed = (
        P("narrow", None, None),
        P("wide", "narrow", None, None),
        P("wide", "narrow", None, None),
        P(),
        P(),
        P("wide"),
    )
    return jax.shard_map(
        per_device,
        mesh=mesh,
        in_specs=placed,
        out_specs=(P("narrow", "wide", None), P()),
        check_vma=False,
    )
```
